32 devices in a mesh: grp: 2 (over x), row: 16 (over z, y, core).
Axes of the slice: x: 2, y: 2, z: 4, core: 2. Of those that a mesh axis runs over, the one named last changes fastest.
Arguments:
- greens: bfloat16 [8192, 16384], P(('grp', 'row')), parts along dimension 0, may hold values from -0.0625 to 0.0625
- track_id: int32 [8192], P(('grp', 'row')), parts along dimension 0, may hold values from 0 to 7
- sigma_inv: float32 [16], P('grp'), parts along dimension 0, may hold values from 1 to 10
- sketch: float32 [192, 128, 128], P('grp', 'row'), parts along dimension 0, may hold values from -6 to 6
Outputs:
- range_basis: float32 [8192, 96], P(('grp', 'row')), parts along dimension 0
- coefficients: float32 [256, 128, 96], P(('grp', 'row')), parts along dimension 0
The draws below stay inside these ranges and needn't reach their ends.
There are 2 independent parts, one for each index of `grp`. The reference program is written for one: setup_inputs(seed, part) draws one part's arguments, and reference() takes and returns one part's arrays. A program takes and returns all parts, laid end to end along the dimension named above; each array names one. Nothing has to cross between parts.
All inputs are finite; a program needn't handle non-finite values.
Results may differ from the reference program's by a relative error of at most 0.011.
Values may be sent and summed in bfloat16 or wider, within the bound.
No kernel may reach another device: no remote copies, remote signals or barrier semaphores. Data moves between devices by JAX's collectives and lax.ppermute only.
A program may use at most 128 MiB of HBM per device.

```python
import math
import jax
import jax.numpy as jnp
from jax import lax

NDIP = 128
NSTRIKE = 128
SKETCH = 96
NTRACK = 8
SWEEPS = 4
ROWS = 4096
PARAMS = 16384


def draw_sketch(key, part):
    common_key = jax.random.fold_in(key, 11)
    column_key = jax.random.fold_in(key, 23)
    common_part = jax.random.normal(common_key, (1, NDIP, NSTRIKE), jnp.float32)
    column_part = jax.random.normal(column_key, (SKETCH, NDIP, NSTRIKE), jnp.float32)
    return jnp.clip(0.95 * common_part + 0.3 * column_part, -6.0, 6.0)


def plant(entries, own_key, smallest, high):
    index_at = [jax.random.randint(jax.random.fold_in(own_key, axis), (), 0, length) for axis, length in enumerate(entries.shape)]
    main_axis = entries.shape.index(max(entries.shape))
    next_to = index_at[:main_axis] + [(index_at[main_axis] + 1) % entries.shape[main_axis]] + index_at[main_axis + 1:]
    return entries.at[tuple(index_at)].set(smallest).at[tuple(next_to)].set(high)


def spiked(drawn, key, source, target, shards_of, factor):
    owner, partner = [(jnp.arange(drawn.shape[position]) // (drawn.shape[position] // shards_of)).reshape([-1 if axis == position else 1 for axis in range(drawn.ndim)]) for position in (source, target)]
    chosen = jax.random.permutation(key, shards_of)[partner]
    strong = (owner == chosen) | (owner == (partner + shards_of // 2) % shards_of)
    return jnp.where(strong, factor * drawn, drawn)


def level_of(rng, shape, split, least, top_value):
    loudness, own = 1.0, jax.random.fold_in(rng, 6)
    for dim, parts in split:
        draws = jnp.exp(jax.random.uniform(jax.random.fold_in(own, dim), (parts,), jnp.float32, least / len(split), top_value / len(split)))
        loudness = loudness * jnp.repeat(draws, shape[dim] // parts).reshape([-1 if axis == dim else 1 for axis in range(len(shape))])
    return loudness


def gaussian_with(own_key, extent, spread, bound, pieces, heavy, kind=jnp.bfloat16):
    values = spread * jax.random.normal(own_key, extent, jnp.float32)
    if pieces:
        values = values * level_of(own_key, extent, pieces, -0.22, 0.18)
    return jnp.clip(spiked(values, jax.random.fold_in(own_key, 3), *heavy), -bound, bound).astype(kind)


def setup_inputs(seed: int = 0, part: int = 0) -> dict:
    key_of = jax.random.split(jax.random.key(seed), 5)
    part_splits = jax.random.split(jax.random.fold_in(key_of[4], part), 5)
    greens = gaussian_with(part_splits[0], (ROWS, PARAMS), PARAMS ** -0.5, 0.0625, ((0, 16),), (0, 1, 16, 2.0))
    track_id = plant(jax.random.randint(part_splits[1], (ROWS,), 0, NTRACK), jax.random.fold_in(part_splits[1], 1), 0, NTRACK - 1).astype(jnp.int32)
    sigma_inv = jnp.clip(jnp.exp(jax.random.uniform(part_splits[2], (NTRACK,), jnp.float32, math.log(1.0), math.log(10.0))), 1.0, 10.0)
    sketch = draw_sketch(jax.random.fold_in(jax.random.fold_in(key_of[4], part), 71), part)
    return dict(greens=greens, track_id=track_id, sigma_inv=sigma_inv, sketch=sketch)


smoothing = 0.24

def smooth_once(field):
    padded = jnp.pad(field, ((0, 0), (1, 1), (1, 1)))
    beside_all = padded[:, 2:, 1:-1] + padded[:, :-2, 1:-1] + padded[:, 1:-1, 2:] + padded[:, 1:-1, :-2]
    return field + smoothing * (beside_all - 4.0 * field)

def orthonormalize(sketched):
    gram_matrix = jnp.dot(sketched.T, sketched, precision=lax.Precision.HIGHEST) / ROWS
    factor = jnp.linalg.cholesky(gram_matrix)
    return lax.linalg.triangular_solve(factor, sketched, left_side=False, lower=True, transpose_a=True)

def reference(greens, track_id, sigma_inv, sketch):
    groups = jnp.arange(NTRACK, dtype=jnp.int32)
    onehot = (track_id[:, None] == groups[None, :]).astype(jnp.float32)
    weights = jnp.dot(onehot, sigma_inv, precision=lax.Precision.HIGHEST)
    field = sketch
    for sweep_index in range(SWEEPS):
        field = smooth_once(field)
    omega = field.reshape(SKETCH, PARAMS).astype(jnp.bfloat16)
    first = lax.dot_general(greens.astype(jnp.float32), omega.astype(jnp.float32), (((1,), (1,)), ((), ())), preferred_element_type=jnp.float32)
    basis_one = orthonormalize(first * weights[:, None])
    weighted_one = (basis_one * weights[:, None]).astype(jnp.bfloat16)
    row_scale = 1.0 / jnp.sqrt(jnp.float32(ROWS))
    back = lax.dot_general(greens.astype(jnp.float32), weighted_one.astype(jnp.float32), (((0,), (0,)), ((), ())), preferred_element_type=jnp.float32)
    back = (back * row_scale).astype(jnp.bfloat16)
    second = jnp.dot(greens.astype(jnp.float32), back.astype(jnp.float32), preferred_element_type=jnp.float32)
    range_basis = orthonormalize(second * weights[:, None])
    weighted_two = (range_basis * weights[:, None]).astype(jnp.bfloat16)
    projected = lax.dot_general(greens.astype(jnp.float32), weighted_two.astype(jnp.float32), (((0,), (0,)), ((), ())), preferred_element_type=jnp.float32)
    coefficients = (projected * row_scale).reshape(NDIP, NSTRIKE, SKETCH)
    return (range_basis, coefficients)
```

```python
import functools

import jax
import jax.numpy as jnp
from jax import lax
from jax.experimental import pallas as pl
from jax.experimental.pallas import tpu as pltpu
from jax.sharding import PartitionSpec as P


SWEEPS = 4
smoothing = 0.24
HIGH = lax.Precision.HIGHEST
f32, bf16 = jnp.float32, jnp.bfloat16
NT = (((1,), (1,)), ((), ()))
VM = pltpu.VMEM


def swap(x, k):
    n = lax.axis_size("row")
    return lax.ppermute(x, "row", [(i, i ^ k) for i in range(n)])


def halo_rows(x, width):
    n, length = lax.axis_size("row"), x.shape[1]
    hops = -(-width // length)
    before, after = [], []
    for hop in range(1, hops + 1):
        take = min(length, width - (hop - 1) * length)
        up = [(i, i + hop) for i in range(n - hop)]
        down = [(j, i) for i, j in up]
        before.insert(0, lax.ppermute(x[:, length - take:], "row", up))
        after.append(lax.ppermute(x[:, :take], "row", down))
    return jnp.concatenate(before, axis=1), jnp.concatenate(after, axis=1)


def smooth_kernel(edge_ref, before_ref, own_ref, after_ref, out_ref):
    columns, length, strike = own_ref.shape
    width = before_ref.shape[1]
    top, bottom = edge_ref[0], edge_ref[1]
    shape = (8, strike)
    lane = lax.broadcasted_iota(jnp.int32, shape, 1)
    from_left = jnp.where(lane == 0, 0.0, smoothing)
    from_right = jnp.where(lane == strike - 1, 0.0, smoothing)
    inside = [jnp.where(jnp.full(shape, i, jnp.int32) >= width - top, 1.0, 0.0) for i in range(width)]
    inside += [None] * length
    inside += [jnp.where(jnp.full(shape, i, jnp.int32) < bottom, 1.0, 0.0) for i in range(width)]

    def group(g, _):
        at = pl.ds(pl.multiple_of(g * 8, 8), 8)
        rows = [before_ref[at, i, :] for i in range(width)]
        rows += [own_ref[at, i, :] for i in range(length)]
        rows += [after_ref[at, i, :] for i in range(width)]
        for sweep in range(width):
            new = list(rows)
            for i in range(sweep + 1, len(rows) - sweep - 1):
                v = rows[i]
                u = v * (1.0 - 4.0 * smoothing) + smoothing * (rows[i + 1] + rows[i - 1])
                u = u + from_left * pltpu.roll(v, 1, 1) + from_right * pltpu.roll(v, strike - 1, 1)
                new[i] = u if inside[i] is None else u * inside[i]
            rows = new
        for i in range(length):
            out_ref[at, i * strike:(i + 1) * strike] = rows[width + i].astype(bf16)
        return 0

    lax.fori_loop(0, columns // 8, group, 0, unroll=2)


def smooth(sketch):
    columns, length, strike = sketch.shape
    n, me = lax.axis_size("row"), lax.axis_index("row")
    before, after = halo_rows(sketch, SWEEPS)
    top = jnp.minimum(me * length, SWEEPS)
    bottom = jnp.minimum((n - 1 - me) * length, SWEEPS)
    return pl.pallas_call(
        smooth_kernel,
        out_shape=jax.ShapeDtypeStruct((columns, length * strike), bf16),
        in_specs=[pl.BlockSpec(memory_space=pltpu.SMEM)] + [pl.BlockSpec(memory_space=VM)] * 3,
        out_specs=pl.BlockSpec(memory_space=VM),
        compiler_params=pltpu.CompilerParams(vmem_limit_bytes=16 << 20),
        name="smooth",
    )(jnp.stack([top, bottom]).astype(jnp.int32), before, sketch, after)


def inverse_kernel(total, gram_ref, out_ref, *, step=8):
    size = gram_ref.shape[0]
    groups = size // 8
    shape = (8, size)
    lane = lax.broadcasted_iota(jnp.int32, shape, 1)
    sub = lax.broadcasted_iota(jnp.int32, shape, 0)
    full = lambda v: jnp.broadcast_to(v, shape)
    rows = [gram_ref[8 * g:8 * g + 8, :] * (1.0 / total) for g in range(groups)]
    scale = [None] * groups
    for j in range(0, size, step):
        g, s = j // 8, j % 8
        below = range(groups - g)
        cols = [[full(rows[g + h][:, j + q:j + q + 1]) for h in below] for q in range(step)]
        block = (lane >= j) & (lane < j + step)
        unit = lambda q: jnp.where(lane == j + q, 1.0, 0.0)
        pivots = [jnp.where(block, unit(q), full(rows[g][s + q:s + q + 1, :])) for q in range(step)]
        p = [[full(cols[t][0][s + q:s + q + 1, :]) for t in range(q + 1)] for q in range(step)]
        rest = [jnp.where(block, 0.0, rows[g + h]) for h in below]
        for q in range(step):
            inv = 1.0 / p[q][q]
            root = lax.rsqrt(p[q][q])
            scale[g] = root if scale[g] is None else jnp.where(sub >= s + q, root, scale[g])
            for r in range(q + 1, step):
                m = p[r][q] * inv
                for t in range(q + 1, r + 1):
                    p[r][t] = p[r][t] - m * p[t][q]
                pivots[r] = pivots[r] - m * pivots[q]
            for h in below:
                f = cols[q][h] * inv
                for t in range(q + 1, step):
                    cols[t][h] = cols[t][h] - f * p[t][q]
                rest[h] = rest[h] - f * pivots[q]
        for h in below:
            rows[g + h] = rest[h] if h else jnp.where(sub < s, rows[g], rest[0])
        for q in range(step):
            rows[g] = jnp.where(sub == s + q, pivots[q], rows[g])
    for g in range(groups):
        index = 8 * g + sub
        lower = jnp.where(lane < index, rows[g], jnp.where(lane == index, 1.0, 0.0))
        out_ref[8 * g:8 * g + 8, :] = lower * scale[g]


def small_call(kernel, outs, args, smem=0, scratch=()):
    spaces = [pltpu.SMEM] * smem + [VM] * (len(args) - smem)
    many = isinstance(outs, list)
    return pl.pallas_call(
        kernel,
        out_shape=outs,
        in_specs=[pl.BlockSpec(memory_space=m) for m in spaces],
        out_specs=[pl.BlockSpec(memory_space=VM)] * len(outs) if many else pl.BlockSpec(memory_space=VM),
        scratch_shapes=list(scratch),
        compiler_params=pltpu.CompilerParams(vmem_limit_bytes=16 << 20),
    )(*args)


def inverse_factor(gram, total):
    return small_call(functools.partial(inverse_kernel, float(total)), jax.ShapeDtypeStruct(gram.shape, f32),
                      [gram])


def copy_blocks(pairs, sem):
    copies = [pltpu.make_async_copy(a, b, sem.at[i]) for i, (a, b) in enumerate(pairs)]
    for c in copies:
        c.start()
    for c in copies:
        c.wait()


def pick_kernel(core_ref, in_ref, out_ref, sem):
    chips, _, block = out_ref.shape
    at = lambda m: pl.ds(pl.multiple_of((2 * m + core_ref[0]) * block, block), block)
    copy_blocks([(in_ref.at[:, at(m)], out_ref.at[m]) for m in range(chips)], sem)


def pick(greens, core, chips, block, out):
    return pl.pallas_call(
        pick_kernel,
        out_shape=out((chips, greens.shape[0], block), greens.dtype),
        in_specs=[pl.BlockSpec(memory_space=pltpu.SMEM), pl.BlockSpec(memory_space=pltpu.HBM)],
        out_specs=pl.BlockSpec(memory_space=VM),
        scratch_shapes=[pltpu.SemaphoreType.DMA((chips,))],
        compiler_params=pltpu.CompilerParams(vmem_limit_bytes=16 << 20),
    )(core[None], greens)


def keep_kernel(in_ref, out_ref, sem):
    copy_blocks([(in_ref.at[m], out_ref.at[m]) for m in range(out_ref.shape[0])], sem)


def keep(x):
    return pl.pallas_call(
        keep_kernel,
        out_shape=VM(x.shape, x.dtype),
        in_specs=[pl.BlockSpec(memory_space=pltpu.HBM)],
        out_specs=pl.BlockSpec(memory_space=VM),
        scratch_shapes=[pltpu.SemaphoreType.DMA((x.shape[0],))],
        compiler_params=pltpu.CompilerParams(vmem_limit_bytes=16 << 20),
        name="keep_theirs",
    )(x)


def forward_kernel(slots, seeded, last, chip_ref, mine_ref, theirs_ref, *refs):
    parts, rest = refs[:len(slots)], refs[len(slots):]
    rows = mine_ref.shape[1]
    a = rest[0][:, :rows] if seeded else 0.0
    b = rest[0][:, rows:] if seeded else 0.0
    for slot, part_ref in zip(slots, parts):
        m = chip_ref[0] ^ slot
        part = part_ref[...]
        a += lax.dot_general(part, mine_ref[m], NT, preferred_element_type=f32)
        b += lax.dot_general(part, theirs_ref[m], NT, preferred_element_type=f32)
    out_ref = rest[1 if seeded else 0]
    out_ref[:, :rows] = a
    out_ref[:, rows:] = b
    if last:
        rest[-1][:, :rows] = b
        rest[-1][:, rows:] = a


def forward_call(chip, mine, theirs, stage, seed, last):
    slots, parts = [s for s, _ in stage], [p for _, p in stage]
    seeds = [] if seed is None else [seed]
    shape = jax.ShapeDtypeStruct((parts[0].shape[0], 2 * mine.shape[1]), f32)
    return small_call(functools.partial(forward_kernel, slots, seed is not None, last),
                      [shape, shape] if last else shape, [chip[None], mine, theirs] + parts + seeds,
                      smem=1)


def finish_kernel(whitened, total_ref, other_ref, weights_ref, *refs):
    y = (total_ref[...] + other_ref[...]) * weights_ref[...]
    if whitened:
        y = jnp.dot(refs[0][...], y, precision=HIGH, preferred_element_type=f32)
    y_ref, weighted_ref, gram_ref = refs[-3:]
    y_ref[...] = y
    weighted_ref[...] = (y * weights_ref[...]).astype(bf16)
    gram_ref[...] = lax.dot_general(y, y, NT, precision=HIGH, preferred_element_type=f32)


def finish(total, other, weights, white):
    columns = total.shape[0]
    outs = [jax.ShapeDtypeStruct(total.shape, f32), jax.ShapeDtypeStruct(total.shape, bf16),
            jax.ShapeDtypeStruct((columns, columns), f32)]
    return small_call(functools.partial(finish_kernel, white is not None), outs,
                      [total, other, weights] + ([] if white is None else [white]))


def backward_kernel(slots, chip_ref, mine_ref, theirs_ref, y_ref, *outs):
    rows = mine_ref.shape[1]
    for slot, out_ref in zip(slots, outs):
        m = chip_ref[0] ^ slot
        v = jnp.dot(y_ref[:, :rows], mine_ref[m], preferred_element_type=f32)
        v += jnp.dot(y_ref[:, rows:], theirs_ref[m], preferred_element_type=f32)
        out_ref[...] = v.astype(out_ref.dtype)


def backward_call(chip, mine, theirs, weighted, slots, dtype):
    shape = jax.ShapeDtypeStruct((weighted.shape[0], mine.shape[2]), dtype)
    return small_call(functools.partial(backward_kernel, slots), [shape] * len(slots),
                      [chip[None], mine, theirs, weighted], smem=1)


def back_kernel(scale, inv_ref, own_ref, *refs):
    total = own_ref[...]
    for r in refs[:-1]:
        total = total + r[...].astype(f32)
    refs[-1][...] = (jnp.dot(inv_ref[...], total, precision=HIGH, preferred_element_type=f32) * scale).astype(bf16)


def order(chips):
    return [0, 2, 6, 4] if chips == 8 else [2 * k for k in range(chips // 2)]


def gram_sum(x, steps):
    for k in steps:
        x = x + swap(x, k)
    return x


def local(greens, track_id, sigma_inv, sketch):
    n = lax.axis_size("row")
    chips = n // 2
    rows, params = greens.shape
    columns, length, strike = sketch.shape
    block = params // n
    total_rows = rows * n
    row_scale = 1.0 / jnp.sqrt(f32(total_rows))
    me = lax.axis_index("row")
    core, chip = me % 2, me // 2

    groups = jnp.arange(sigma_inv.shape[0], dtype=jnp.int32)
    onehot = (track_id[:, None] == groups[None, :]).astype(f32)
    weights = jnp.dot(onehot, sigma_inv, precision=HIGH)
    weights = jnp.concatenate([weights, swap(weights, 1)])

    weights = weights[None, :]
    omega = smooth(sketch)
    sent = pick(pltpu.with_memory_space_constraint(greens, pltpu.HBM), 1 - core, chips, block,
                jax.ShapeDtypeStruct)
    theirs = swap(sent, 1)
    theirs = keep(theirs)
    mine = pick(pltpu.with_memory_space_constraint(greens, pltpu.HBM), core, chips, block, VM)

    def forward(own):
        near, ks = {}, order(chips)
        for k in ks:
            near[k] = own if k == 0 else swap(own, 2 * k)
        across = {k: swap(near[k], 2) for k in ks}
        stages = [[(k, near[k]) for k in ks[:-1]] + [(k + 1, across[k]) for k in ks[:-2]],
                  [(k, near[k]) for k in ks[-1:]] + [(k + 1, across[k]) for k in ks[-2:-1]],
                  [(ks[-1] + 1, across[ks[-1]])]]
        total = None
        for i, stage in enumerate(stages):
            total = forward_call(chip, mine, theirs, stage, total, i == len(stages) - 1)
        return total[0], swap(total[1], 1)

    def backward(weighted):
        ks = order(chips)[::-1]

        def call(slots, dtype):
            return backward_call(chip, mine, theirs, weighted, slots, dtype)

        sent = call([ks[0] + 1], bf16) + call([k + 1 for k in ks[1:]], bf16)
        kept = call(ks, f32)
        sums = [a + swap(v, 2).astype(f32) for a, v in zip(kept, sent)]
        far = [swap(v.astype(bf16), 2 * k) for v, k in zip(sums, ks) if k]
        return [sums[-1]] + far

    slower = [1 << i for i in range(2, n.bit_length() - 1)]
    gram0 = gram_sum(lax.dot_general(omega, omega, NT, preferred_element_type=f32), [1, 2] + slower)
    white = inverse_factor(gram0, params)
    _, weighted, gram = finish(*forward(omega), weights, white)
    pieces = backward(weighted)
    inv_one = inverse_factor(gram_sum(gram, slower + [2]), total_rows)
    back = small_call(functools.partial(back_kernel, float(total_rows) ** -0.5),
                      jax.ShapeDtypeStruct((columns, block), bf16), [inv_one] + pieces)
    second, weighted, gram = finish(*forward(back), weights, None)
    pieces = backward(weighted)
    inv_two = inverse_factor(gram_sum(gram, slower + [2]), total_rows)
    projected = sum([v.astype(f32) for v in pieces[1:]], pieces[0])
    range_basis = lax.dot_general(second[:, :rows], inv_two, (((0,), (1,)), ((), ())), precision=HIGH)
    coefficients = lax.dot_general(projected, inv_two, (((0,), (1,)), ((), ())), precision=HIGH) * row_scale
    return (range_basis, coefficients.reshape(length, strike, columns))


def solution(mesh):
    in_specs = (P(("grp", "row"), None), P(("grp", "row")), P("grp"), P("grp", "row", None))
    out_specs = (P(("grp", "row"), None), P(("grp", "row"), None, None))

    return jax.shard_map(local, mesh=mesh, in_specs=in_specs, out_specs=out_specs, check_vma=False)
```

```python
import functools

import jax
import jax.numpy as jnp
from jax import lax
from jax.experimental import pallas as pl
from jax.experimental.pallas import tpu as pltpu
from jax.sharding import PartitionSpec as P


SWEEPS = 4
smoothing = 0.24
HIGH = lax.Precision.HIGHEST
f32, bf16 = jnp.float32, jnp.bfloat16
NT = (((1,), (1,)), ((), ()))
VM = pltpu.VMEM


def swap(x, k):
    n = lax.axis_size("row")
    return lax.ppermute(x, "row", [(i, i ^ k) for i in range(n)])


def halo_rows(x, width):
    n, length = lax.axis_size("row"), x.shape[1]
    hops = -(-width // length)
    before, after = [], []
    for hop in range(1, hops + 1):
        take = min(length, width - (hop - 1) * length)
        up = [(i, i + hop) for i in range(n - hop)]
        down = [(j, i) for i, j in up]
        before.insert(0, lax.ppermute(x[:, length - take:], "row", up))
        after.append(lax.ppermute(x[:, :take], "row", down))
    return jnp.concatenate(before, axis=1), jnp.concatenate(after, axis=1)


def smooth_kernel(edge_ref, before_ref, own_ref, after_ref, out_ref):
    columns, length, strike = own_ref.shape
    width = before_ref.shape[1]
    top, bottom = edge_ref[0], edge_ref[1]
    shape = (8, strike)
    lane = lax.broadcasted_iota(jnp.int32, shape, 1)
    from_left = jnp.where(lane == 0, 0.0, smoothing)
    from_right = jnp.where(lane == strike - 1, 0.0, smoothing)
    inside = [jnp.where(jnp.full(shape, i, jnp.int32) >= width - top, 1.0, 0.0) for i in range(width)]
    inside += [None] * length
    inside += [jnp.where(jnp.full(shape, i, jnp.int32) < bottom, 1.0, 0.0) for i in range(width)]

    def group(g, _):
        at = pl.ds(pl.multiple_of(g * 8, 8), 8)
        rows = [before_ref[at, i, :] for i in range(width)]
        rows += [own_ref[at, i, :] for i in range(length)]
        rows += [after_ref[at, i, :] for i in range(width)]
        for sweep in range(width):
            new = list(rows)
            for i in range(sweep + 1, len(rows) - sweep - 1):
                v = rows[i]
                u = v * (1.0 - 4.0 * smoothing) + smoothing * (rows[i + 1] + rows[i - 1])
                u = u + from_left * pltpu.roll(v, 1, 1) + from_right * pltpu.roll(v, strike - 1, 1)
                new[i] = u if inside[i] is None else u * inside[i]
            rows = new
        for i in range(length):
            out_ref[at, i * strike:(i + 1) * strike] = rows[width + i].astype(bf16)
        return 0

    lax.fori_loop(0, columns // 8, group, 0, unroll=2)


def smooth(sketch):
    columns, length, strike = sketch.shape
    n, me = lax.axis_size("row"), lax.axis_index("row")
    before, after = halo_rows(sketch, SWEEPS)
    top = jnp.minimum(me * length, SWEEPS)
    bottom = jnp.minimum((n - 1 - me) * length, SWEEPS)
    return pl.pallas_call(
        smooth_kernel,
        out_shape=jax.ShapeDtypeStruct((columns, length * strike), bf16),
        in_specs=[pl.BlockSpec(memory_space=pltpu.SMEM)] + [pl.BlockSpec(memory_space=VM)] * 3,
        out_specs=pl.BlockSpec(memory_space=VM),
        compiler_params=pltpu.CompilerParams(vmem_limit_bytes=16 << 20),
        name="smooth",
    )(jnp.stack([top, bottom]).astype(jnp.int32), before, sketch, after)


def eliminate(rows, out_ref, step=8):
    groups, size = len(rows), rows[0].shape[1]
    shape = (8, size)
    lane = lax.broadcasted_iota(jnp.int32, shape, 1)
    sub = lax.broadcasted_iota(jnp.int32, shape, 0)
    full = lambda v: jnp.broadcast_to(v, shape)
    scale = [None] * groups
    for j in range(0, size, step):
        g, s = j // 8, j % 8
        below = range(groups - g)
        cols = [[full(rows[g + h][:, j + q:j + q + 1]) for h in below] for q in range(step)]
        block = (lane >= j) & (lane < j + step)
        unit = lambda q: jnp.where(lane == j + q, 1.0, 0.0)
        pivots = [jnp.where(block, unit(q), full(rows[g][s + q:s + q + 1, :])) for q in range(step)]
        p = [[full(cols[t][0][s + q:s + q + 1, :]) for t in range(q + 1)] for q in range(step)]
        rest = [jnp.where(block, 0.0, rows[g + h]) for h in below]
        for q in range(step):
            inv = 1.0 / p[q][q]
            root = lax.rsqrt(p[q][q])
            scale[g] = root if scale[g] is None else jnp.where(sub >= s + q, root, scale[g])
            for r in range(q + 1, step):
                m = p[r][q] * inv
                for t in range(q + 1, r + 1):
                    p[r][t] = p[r][t] - m * p[t][q]
                pivots[r] = pivots[r] - m * pivots[q]
            for h in below:
                f = cols[q][h] * inv
                for t in range(q + 1, step):
                    cols[t][h] = cols[t][h] - f * p[t][q]
                rest[h] = rest[h] - f * pivots[q]
        for h in below:
            rows[g + h] = rest[h] if h else jnp.where(sub < s, rows[g], rest[0])
        for q in range(step):
            rows[g] = jnp.where(sub == s + q, pivots[q], rows[g])
    for g in range(groups):
        index = 8 * g + sub
        lower = jnp.where(lane < index, rows[g], jnp.where(lane == index, 1.0, 0.0))
        out_ref[8 * g:8 * g + 8, :] = lower * scale[g]


def inverse_kernel(total, gram_ref, out_ref):
    size = gram_ref.shape[0]
    eliminate([gram_ref[g:g + 8, :] * (1.0 / total) for g in range(0, size, 8)], out_ref)


def small_call(kernel, outs, args, smem=0, scratch=()):
    spaces = [pltpu.SMEM] * smem + [VM] * (len(args) - smem)
    many = isinstance(outs, list)
    return pl.pallas_call(
        kernel,
        out_shape=outs,
        in_specs=[pl.BlockSpec(memory_space=m) for m in spaces],
        out_specs=[pl.BlockSpec(memory_space=VM)] * len(outs) if many else pl.BlockSpec(memory_space=VM),
        scratch_shapes=list(scratch),
        compiler_params=pltpu.CompilerParams(vmem_limit_bytes=16 << 20),
    )(*args)


def inverse_factor(gram, total):
    return small_call(functools.partial(inverse_kernel, float(total)), jax.ShapeDtypeStruct(gram.shape, f32),
                      [gram])


def copy_blocks(pairs, sem):
    copies = [pltpu.make_async_copy(a, b, sem.at[i]) for i, (a, b) in enumerate(pairs)]
    for c in copies:
        c.start()
    for c in copies:
        c.wait()


def pick_kernel(core_ref, in_ref, out_ref, sem):
    chips, _, block = out_ref.shape
    at = lambda m: pl.ds(pl.multiple_of((2 * m + core_ref[0]) * block, block), block)
    copy_blocks([(in_ref.at[:, at(m)], out_ref.at[m]) for m in range(chips)], sem)


def pick(greens, core, chips, block, out):
    return pl.pallas_call(
        pick_kernel,
        out_shape=out((chips, greens.shape[0], block), greens.dtype),
        in_specs=[pl.BlockSpec(memory_space=pltpu.SMEM), pl.BlockSpec(memory_space=pltpu.HBM)],
        out_specs=pl.BlockSpec(memory_space=VM),
        scratch_shapes=[pltpu.SemaphoreType.DMA((chips,))],
        compiler_params=pltpu.CompilerParams(vmem_limit_bytes=16 << 20),
    )(core[None], greens)


def keep_kernel(in_ref, out_ref, sem):
    copy_blocks([(in_ref.at[m], out_ref.at[m]) for m in range(out_ref.shape[0])], sem)


def keep(x):
    return pl.pallas_call(
        keep_kernel,
        out_shape=VM(x.shape, x.dtype),
        in_specs=[pl.BlockSpec(memory_space=pltpu.HBM)],
        out_specs=pl.BlockSpec(memory_space=VM),
        scratch_shapes=[pltpu.SemaphoreType.DMA((x.shape[0],))],
        compiler_params=pltpu.CompilerParams(vmem_limit_bytes=16 << 20),
        name="keep_theirs",
    )(x)


def forward_kernel(slots, seeded, last, whiten, chip_ref, mine_ref, theirs_ref, *refs):
    parts, rest = refs[:len(slots)], refs[len(slots):]
    rows, columns = mine_ref.shape[1], parts[0].shape[0]
    take = (pl.ds(0, rows), pl.ds(rows, rows), pl.ds(2 * rows, columns))[:2 + whiten]
    sums = [rest[0][:, t] if seeded else 0.0 for t in take]
    for slot, part_ref in zip(slots, parts):
        m = chip_ref[0] ^ slot
        part = part_ref[...]
        for i, other in enumerate((mine_ref[m], theirs_ref[m], part)[:len(take)]):
            sums[i] += lax.dot_general(part, other, NT, preferred_element_type=f32)
    outs = [(rest[1 if seeded else 0], sums)]
    if last:
        outs.append((rest[-1], [sums[1], sums[0]] + sums[2:]))
    for ref, values in outs:
        for t, v in zip(take, values):
            ref[:, t] = v


def forward_call(chip, mine, theirs, stage, seed, last, whiten):
    slots, parts = [s for s, _ in stage], [p for _, p in stage]
    seeds = [] if seed is None else [seed]
    columns, width = parts[0].shape[0], 2 * mine.shape[1]
    if whiten:
        width += -(-columns // 128) * 128
    shape = jax.ShapeDtypeStruct((columns, width), f32)
    return small_call(functools.partial(forward_kernel, slots, seed is not None, last, whiten),
                      [shape, shape] if last else shape, [chip[None], mine, theirs] + parts + seeds,
                      smem=1)


def finish_kernel(params, total_ref, other_ref, weights_ref, y_ref, weighted_ref, gram_ref, *scratch):
    width, columns = y_ref.shape[1], y_ref.shape[0]
    y = (total_ref[:, :width] + other_ref[:, :width]) * weights_ref[...]
    if params:
        at = lambda g: (pl.ds(g, 8), pl.ds(width, columns))
        eliminate([(total_ref[at(g)] + other_ref[at(g)]) * (1.0 / params) for g in range(0, columns, 8)], scratch[0])
        y = jnp.dot(scratch[0][...], y, precision=HIGH, preferred_element_type=f32)
    y_ref[...] = y
    weighted_ref[...] = (y * weights_ref[...]).astype(bf16)
    gram_ref[...] = lax.dot_general(y, y, NT, precision=HIGH, preferred_element_type=f32)


def finish(total, other, weights, params):
    columns, width = total.shape[0], weights.shape[1]
    outs = [jax.ShapeDtypeStruct((columns, width), f32), jax.ShapeDtypeStruct((columns, width), bf16),
            jax.ShapeDtypeStruct((columns, columns), f32)]
    return small_call(functools.partial(finish_kernel, params), outs, [total, other, weights],
                      scratch=[VM((columns, columns), f32)] if params else [])


def backward_kernel(slots, chip_ref, mine_ref, theirs_ref, y_ref, *outs):
    rows = mine_ref.shape[1]
    for slot, out_ref in zip(slots, outs):
        m = chip_ref[0] ^ slot
        v = jnp.dot(y_ref[:, :rows], mine_ref[m], preferred_element_type=f32)
        v += jnp.dot(y_ref[:, rows:], theirs_ref[m], preferred_element_type=f32)
        out_ref[...] = v.astype(out_ref.dtype)


def backward_call(chip, mine, theirs, weighted, slots, dtype):
    shape = jax.ShapeDtypeStruct((weighted.shape[0], mine.shape[2]), dtype)
    return small_call(functools.partial(backward_kernel, slots), [shape] * len(slots),
                      [chip[None], mine, theirs, weighted], smem=1)


def back_kernel(scale, inv_ref, own_ref, *refs):
    total = own_ref[...]
    for r in refs[:-1]:
        total = total + r[...].astype(f32)
    refs[-1][...] = (jnp.dot(inv_ref[...], total, precision=HIGH, preferred_element_type=f32) * scale).astype(bf16)


def project_kernel(scale, inv_ref, own_ref, *refs):
    total = own_ref[...]
    for r in refs[:-1]:
        total = total + r[...].astype(f32)
    out = jnp.dot(inv_ref[...], total, precision=HIGH, preferred_element_type=f32) * scale
    length, _, strike = refs[-1].shape
    for i in range(length):
        refs[-1][i] = out[:, i * strike:(i + 1) * strike]


def order(chips):
    return [0, 2, 6, 4] if chips == 8 else [2 * k for k in range(chips // 2)]


def direct(n):
    return n <= 16 and n & (n - 1) == 0


def same_core():
    n = lax.axis_size("row")
    return [list(range(core, n, 2)) for core in range(2)]


def gram_sum(x):
    n = lax.axis_size("row")
    if not direct(n):
        return lax.psum(x, "row", axis_index_groups=same_core())
    far = [swap(x, 4 * k) for k in range(1, n // 4)]
    x = sum(far, x)
    return x + swap(x, 2)


def local(greens, track_id, sigma_inv, sketch):
    n = lax.axis_size("row")
    chips = n // 2
    rows, params = greens.shape
    columns, length, strike = sketch.shape
    block = params // n
    total_rows = rows * n
    me = lax.axis_index("row")
    core, chip = me % 2, me // 2

    groups = jnp.arange(sigma_inv.shape[0], dtype=jnp.int32)
    onehot = (track_id[:, None] == groups[None, :]).astype(f32)
    weights = jnp.dot(onehot, sigma_inv, precision=HIGH)
    weights = jnp.concatenate([weights, swap(weights, 1)])

    weights = weights[None, :]
    omega = smooth(sketch)
    sent = pick(pltpu.with_memory_space_constraint(greens, pltpu.HBM), 1 - core, chips, block,
                jax.ShapeDtypeStruct)
    theirs = swap(sent, 1)
    theirs = keep(theirs)
    mine = pick(pltpu.with_memory_space_constraint(greens, pltpu.HBM), core, chips, block, VM)

    def forward(own, whiten):
        if not direct(n):
            parts = lax.all_gather(own, "row", axis_index_groups=same_core())
            stage = [(m, parts[m]) for m in range(chips)]
            total = forward_call(0 * chip, mine, theirs, stage, None, True, whiten)
            return total[0], swap(total[1], 1)
        near, ks = {}, order(chips)
        for k in ks:
            near[k] = own if k == 0 else swap(own, 2 * k)
        across = {k: swap(near[k], 2) for k in ks}
        stages = [[(k, near[k]) for k in ks[:-1]] + [(k + 1, across[k]) for k in ks[:-2]],
                  [(k, near[k]) for k in ks[-1:]] + [(k + 1, across[k]) for k in ks[-2:-1]],
                  [(ks[-1] + 1, across[ks[-1]])]]
        total = None
        for i, stage in enumerate(stages):
            total = forward_call(chip, mine, theirs, stage, total, i == len(stages) - 1, whiten)
        return total[0], swap(total[1], 1)

    def backward(weighted):
        if not direct(n):
            every = backward_call(0 * chip, mine, theirs, weighted, list(range(chips)), f32)
            return [lax.psum_scatter(jnp.stack(every), "row", axis_index_groups=same_core())]
        ks = order(chips)[::-1]

        def call(slots, dtype):
            return backward_call(chip, mine, theirs, weighted, slots, dtype)

        sent = call([ks[0] + 1], bf16) + call([k + 1 for k in ks[1:]], bf16)
        kept = call(ks, f32)
        sums = [a + swap(v, 2).astype(f32) for a, v in zip(kept, sent)]
        far = [swap(v.astype(bf16), 2 * k) for v, k in zip(sums, ks) if k]
        return [sums[-1]] + far

    _, weighted, gram = finish(*forward(omega, True), weights, float(params))
    pieces = backward(weighted)
    inv_one = inverse_factor(gram_sum(gram), total_rows)
    back = small_call(functools.partial(back_kernel, float(total_rows) ** -0.5),
                      jax.ShapeDtypeStruct((columns, block), bf16), [inv_one] + pieces)
    second, weighted, gram = finish(*forward(back, False), weights, None)
    pieces = backward(weighted)
    inv_two = inverse_factor(gram_sum(gram), total_rows)
    range_basis = lax.dot_general(second[:, :rows], inv_two, (((0,), (1,)), ((), ())), precision=HIGH)
    coefficients = small_call(functools.partial(project_kernel, float(total_rows) ** -0.5),
                              jax.ShapeDtypeStruct((length, columns, strike), f32), [inv_two] + pieces)
    return (range_basis, coefficients.transpose(0, 2, 1))


def solution(mesh):
    in_specs = (P(("grp", "row"), None), P(("grp", "row")), P("grp"), P("grp", "row", None))
    out_specs = (P(("grp", "row"), None), P(("grp", "row"), None, None))

    return jax.shard_map(local, mesh=mesh, in_specs=in_specs, out_specs=out_specs, check_vma=False)
```

```python
import functools

import jax
import jax.numpy as jnp
from jax import lax
from jax.experimental import pallas as pl
from jax.experimental.pallas import tpu as pltpu
from jax.sharding import PartitionSpec as P


SWEEPS = 4
smoothing = 0.24
HIGH = lax.Precision.HIGHEST
f32, bf16 = jnp.float32, jnp.bfloat16
NT = (((1,), (1,)), ((), ()))
VM = pltpu.VMEM


def swap(x, k):
    n = lax.axis_size("row")
    return lax.ppermute(x, "row", [(i, i ^ k) for i in range(n)])


def halo_rows(x, width):
    n, length = lax.axis_size("row"), x.shape[1]
    hops = -(-width // length)
    before, after = [], []
    for hop in range(1, hops + 1):
        take = min(length, width - (hop - 1) * length)
        up = [(i, i + hop) for i in range(n - hop)]
        down = [(j, i) for i, j in up]
        before.insert(0, lax.ppermute(x[:, length - take:], "row", up))
        after.append(lax.ppermute(x[:, :take], "row", down))
    return jnp.concatenate(before, axis=1), jnp.concatenate(after, axis=1)


def smooth_kernel(edge_ref, before_ref, own_ref, after_ref, out_ref):
    columns, length, strike = own_ref.shape
    width = before_ref.shape[1]
    top, bottom = edge_ref[0], edge_ref[1]
    shape = (8, strike)
    lane = lax.broadcasted_iota(jnp.int32, shape, 1)
    from_left = jnp.where(lane == 0, 0.0, smoothing)
    from_right = jnp.where(lane == strike - 1, 0.0, smoothing)
    inside = [jnp.where(jnp.full(shape, i, jnp.int32) >= width - top, 1.0, 0.0) for i in range(width)]
    inside += [None] * length
    inside += [jnp.where(jnp.full(shape, i, jnp.int32) < bottom, 1.0, 0.0) for i in range(width)]

    def group(g, _):
        at = pl.ds(pl.multiple_of(g * 8, 8), 8)
        rows = [before_ref[at, i, :] for i in range(width)]
        rows += [own_ref[at, i, :] for i in range(length)]
        rows += [after_ref[at, i, :] for i in range(width)]
        for sweep in range(width):
            new = list(rows)
            for i in range(sweep + 1, len(rows) - sweep - 1):
                v = rows[i]
                u = v * (1.0 - 4.0 * smoothing) + smoothing * (rows[i + 1] + rows[i - 1])
                u = u + from_left * pltpu.roll(v, 1, 1) + from_right * pltpu.roll(v, strike - 1, 1)
                new[i] = u if inside[i] is None else u * inside[i]
            rows = new
        for i in range(length):
            out_ref[at, i * strike:(i + 1) * strike] = rows[width + i].astype(bf16)
        return 0

    lax.fori_loop(0, columns // 8, group, 0, unroll=4)


def smooth(sketch):
    columns, length, strike = sketch.shape
    n, me = lax.axis_size("row"), lax.axis_index("row")
    before, after = halo_rows(sketch, SWEEPS)
    top = jnp.minimum(me * length, SWEEPS)
    bottom = jnp.minimum((n - 1 - me) * length, SWEEPS)
    return pl.pallas_call(
        smooth_kernel,
        out_shape=jax.ShapeDtypeStruct((columns, length * strike), bf16),
        in_specs=[pl.BlockSpec(memory_space=pltpu.SMEM)] + [pl.BlockSpec(memory_space=VM)] * 3,
        out_specs=pl.BlockSpec(memory_space=VM),
        compiler_params=pltpu.CompilerParams(vmem_limit_bytes=16 << 20),
        name="smooth",
    )(jnp.stack([top, bottom]).astype(jnp.int32), before, sketch, after)


def eliminate(rows, out_ref, step=8):
    groups, size = len(rows), rows[0].shape[1]
    shape = (8, size)
    lane = lax.broadcasted_iota(jnp.int32, shape, 1)
    sub = lax.broadcasted_iota(jnp.int32, shape, 0)
    full = lambda v: jnp.broadcast_to(v, shape)
    scale = [None] * groups
    for j in range(0, size, step):
        g, s = j // 8, j % 8
        below = range(groups - g)
        cols = [[full(rows[g + h][:, j + q:j + q + 1]) for h in below] for q in range(step)]
        block = (lane >= j) & (lane < j + step)
        unit = lambda q: jnp.where(lane == j + q, 1.0, 0.0)
        pivots = [jnp.where(block, unit(q), full(rows[g][s + q:s + q + 1, :])) for q in range(step)]
        p = [[full(cols[t][0][s + q:s + q + 1, :]) for t in range(q + 1)] for q in range(step)]
        rest = [jnp.where(block, 0.0, rows[g + h]) for h in below]
        for q in range(step):
            inv = 1.0 / p[q][q]
            root = lax.rsqrt(p[q][q])
            scale[g] = root if scale[g] is None else jnp.where(sub >= s + q, root, scale[g])
            for r in range(q + 1, step):
                m = p[r][q] * inv
                for t in range(q + 1, r + 1):
                    p[r][t] = p[r][t] - m * p[t][q]
                pivots[r] = pivots[r] - m * pivots[q]
            for h in below:
                f = cols[q][h] * inv
                for t in range(q + 1, step):
                    cols[t][h] = cols[t][h] - f * p[t][q]
                rest[h] = rest[h] - f * pivots[q]
        for h in below:
            rows[g + h] = rest[h] if h else jnp.where(sub < s, rows[g], rest[0])
        for q in range(step):
            rows[g] = jnp.where(sub == s + q, pivots[q], rows[g])
    for g in range(groups):
        index = 8 * g + sub
        lower = jnp.where(lane < index, rows[g], jnp.where(lane == index, 1.0, 0.0))
        out_ref[8 * g:8 * g + 8, :] = lower * scale[g]


def inverse_kernel(total, gram_ref, out_ref):
    size = gram_ref.shape[0]
    eliminate([gram_ref[g:g + 8, :] * (1.0 / total) for g in range(0, size, 8)], out_ref)


def small_call(kernel, outs, args, smem=0, scratch=()):
    spaces = [pltpu.SMEM] * smem + [VM] * (len(args) - smem)
    many = isinstance(outs, list)
    return pl.pallas_call(
        kernel,
        out_shape=outs,
        in_specs=[pl.BlockSpec(memory_space=m) for m in spaces],
        out_specs=[pl.BlockSpec(memory_space=VM)] * len(outs) if many else pl.BlockSpec(memory_space=VM),
        scratch_shapes=list(scratch),
        compiler_params=pltpu.CompilerParams(vmem_limit_bytes=16 << 20),
    )(*args)


def inverse_factor(gram, total):
    return small_call(functools.partial(inverse_kernel, float(total)), jax.ShapeDtypeStruct(gram.shape, f32),
                      [gram])


def copy_blocks(pairs, sem):
    copies = [pltpu.make_async_copy(a, b, sem.at[i]) for i, (a, b) in enumerate(pairs)]
    for c in copies:
        c.start()
    for c in copies:
        c.wait()


def pick_kernel(core_ref, in_ref, out_ref, sem):
    chips, _, block = out_ref.shape
    at = lambda m: pl.ds(pl.multiple_of((2 * m + core_ref[0]) * block, block), block)
    copy_blocks([(in_ref.at[:, at(m)], out_ref.at[m]) for m in range(chips)], sem)


def pick(greens, core, chips, block, out):
    return pl.pallas_call(
        pick_kernel,
        out_shape=out((chips, greens.shape[0], block), greens.dtype),
        in_specs=[pl.BlockSpec(memory_space=pltpu.SMEM), pl.BlockSpec(memory_space=pltpu.HBM)],
        out_specs=pl.BlockSpec(memory_space=VM),
        scratch_shapes=[pltpu.SemaphoreType.DMA((chips,))],
        compiler_params=pltpu.CompilerParams(vmem_limit_bytes=16 << 20),
    )(core[None], greens)


def keep_kernel(in_ref, out_ref, sem):
    copy_blocks([(in_ref.at[m], out_ref.at[m]) for m in range(out_ref.shape[0])], sem)


def keep(x):
    return pl.pallas_call(
        keep_kernel,
        out_shape=VM(x.shape, x.dtype),
        in_specs=[pl.BlockSpec(memory_space=pltpu.HBM)],
        out_specs=pl.BlockSpec(memory_space=VM),
        scratch_shapes=[pltpu.SemaphoreType.DMA((x.shape[0],))],
        compiler_params=pltpu.CompilerParams(vmem_limit_bytes=16 << 20),
        name="keep_theirs",
    )(x)


def forward_kernel(slots, seeded, last, whiten, chip_ref, mine_ref, theirs_ref, *refs):
    parts, rest = refs[:len(slots)], refs[len(slots):]
    rows, columns = mine_ref.shape[1], parts[0].shape[0]
    take = (pl.ds(0, rows), pl.ds(rows, rows), pl.ds(2 * rows, columns))[:2 + whiten]
    sums = [rest[0][:, t] if seeded else 0.0 for t in take]
    for slot, part_ref in zip(slots, parts):
        m = chip_ref[0] ^ slot
        part = part_ref[...]
        for i, other in enumerate((mine_ref[m], theirs_ref[m], part)[:len(take)]):
            sums[i] += lax.dot_general(part, other, NT, preferred_element_type=f32)
    outs = [(rest[1 if seeded else 0], sums)]
    if last:
        outs.append((rest[-1], [sums[1], sums[0]] + sums[2:]))
    for ref, values in outs:
        for t, v in zip(take, values):
            ref[:, t] = v


def forward_call(chip, mine, theirs, stage, seed, last, whiten):
    slots, parts = [s for s, _ in stage], [p for _, p in stage]
    seeds = [] if seed is None else [seed]
    columns, width = parts[0].shape[0], 2 * mine.shape[1]
    if whiten:
        width += -(-columns // 128) * 128
    shape = jax.ShapeDtypeStruct((columns, width), f32)
    return small_call(functools.partial(forward_kernel, slots, seed is not None, last, whiten),
                      [shape, shape] if last else shape, [chip[None], mine, theirs] + parts + seeds,
                      smem=1)


def finish_kernel(params, total_ref, other_ref, weights_ref, y_ref, weighted_ref, gram_ref, *scratch):
    width, columns = y_ref.shape[1], y_ref.shape[0]
    y = (total_ref[:, :width] + other_ref[:, :width]) * weights_ref[...]
    if params:
        at = lambda g: (pl.ds(g, 8), pl.ds(width, columns))
        eliminate([(total_ref[at(g)] + other_ref[at(g)]) * (1.0 / params) for g in range(0, columns, 8)], scratch[0])
        y = jnp.dot(scratch[0][...], y, precision=HIGH, preferred_element_type=f32)
    y_ref[...] = y
    weighted_ref[...] = (y * weights_ref[...]).astype(bf16)
    gram_ref[...] = lax.dot_general(y, y, NT, precision=HIGH, preferred_element_type=f32)


def finish(total, other, weights, params):
    columns, width = total.shape[0], weights.shape[1]
    outs = [jax.ShapeDtypeStruct((columns, width), f32), jax.ShapeDtypeStruct((columns, width), bf16),
            jax.ShapeDtypeStruct((columns, columns), f32)]
    return small_call(functools.partial(finish_kernel, params), outs, [total, other, weights],
                      scratch=[VM((columns, columns), f32)] if params else [])


def backward_kernel(slots, chip_ref, mine_ref, theirs_ref, y_ref, *outs):
    rows = mine_ref.shape[1]
    for slot, out_ref in zip(slots, outs):
        m = chip_ref[0] ^ slot
        v = jnp.dot(y_ref[:, :rows], mine_ref[m], preferred_element_type=f32)
        v += jnp.dot(y_ref[:, rows:], theirs_ref[m], preferred_element_type=f32)
        out_ref[...] = v.astype(out_ref.dtype)


def backward_call(chip, mine, theirs, weighted, slots, dtype):
    shape = jax.ShapeDtypeStruct((weighted.shape[0], mine.shape[2]), dtype)
    return small_call(functools.partial(backward_kernel, slots), [shape] * len(slots),
                      [chip[None], mine, theirs, weighted], smem=1)


def back_kernel(scale, inv_ref, own_ref, *refs):
    total = own_ref[...]
    for r in refs[:-1]:
        total = total + r[...].astype(f32)
    refs[-1][...] = (jnp.dot(inv_ref[...], total, precision=HIGH, preferred_element_type=f32) * scale).astype(bf16)


def project_kernel(scale, inv_ref, own_ref, *refs):
    total = own_ref[...]
    for r in refs[:-1]:
        total = total + r[...].astype(f32)
    out = jnp.dot(inv_ref[...], total, precision=HIGH, preferred_element_type=f32) * scale
    length, _, strike = refs[-1].shape
    for i in range(length):
        refs[-1][i] = out[:, i * strike:(i + 1) * strike]


def order(chips):
    return [0, 2, 6, 4] if chips == 8 else [2 * k for k in range(chips // 2)]


def direct(n):
    return n <= 16 and n & (n - 1) == 0


def same_core():
    n = lax.axis_size("row")
    return [list(range(core, n, 2)) for core in range(2)]


def gram_sum(x):
    n = lax.axis_size("row")
    if not direct(n):
        return lax.psum(x, "row", axis_index_groups=same_core())
    far = [swap(x, 2 * k) for k in order(n // 2)[::-1] if k]
    x = sum(far, x)
    return x + swap(x, 2)


def local(greens, track_id, sigma_inv, sketch):
    n = lax.axis_size("row")
    chips = n // 2
    rows, params = greens.shape
    columns, length, strike = sketch.shape
    block = params // n
    total_rows = rows * n
    me = lax.axis_index("row")
    core, chip = me % 2, me // 2

    groups = jnp.arange(sigma_inv.shape[0], dtype=jnp.int32)
    onehot = (track_id[:, None] == groups[None, :]).astype(f32)
    weights = jnp.dot(onehot, sigma_inv, precision=HIGH)
    weights = jnp.concatenate([weights, swap(weights, 1)])

    weights = weights[None, :]
    omega = smooth(sketch)
    sent = pick(pltpu.with_memory_space_constraint(greens, pltpu.HBM), 1 - core, chips, block,
                jax.ShapeDtypeStruct)
    theirs = swap(sent, 1)
    theirs = keep(theirs)
    mine = pick(pltpu.with_memory_space_constraint(greens, pltpu.HBM), core, chips, block, VM)

    def forward(own, whiten):
        if not direct(n):
            parts = lax.all_gather(own, "row", axis_index_groups=same_core())
            stage = [(m, parts[m]) for m in range(chips)]
            total = forward_call(0 * chip, mine, theirs, stage, None, True, whiten)
            return total[0], swap(total[1], 1)
        near, ks = {}, order(chips)
        for k in ks:
            near[k] = own if k == 0 else swap(own, 2 * k)
        across = {k: swap(near[k], 2) for k in ks}
        stages = [[(k, near[k]) for k in ks[:-1]] + [(k + 1, across[k]) for k in ks[:-2]],
                  [(k, near[k]) for k in ks[-1:]] + [(k + 1, across[k]) for k in ks[-2:-1]],
                  [(ks[-1] + 1, across[ks[-1]])]]
        total = None
        for i, stage in enumerate(stages):
            total = forward_call(chip, mine, theirs, stage, total, i == len(stages) - 1, whiten)
        return total[0], swap(total[1], 1)

    def backward(weighted):
        if not direct(n):
            every = backward_call(0 * chip, mine, theirs, weighted, list(range(chips)), f32)
            return [lax.psum_scatter(jnp.stack(every), "row", axis_index_groups=same_core())]
        ks = order(chips)[::-1]

        def call(slots, dtype):
            return backward_call(chip, mine, theirs, weighted, slots, dtype)

        sent = call([ks[0] + 1], bf16) + call([k + 1 for k in ks[1:]], bf16)
        kept = call(ks, f32)
        far = []
        for a, v, k in zip(kept, sent, ks):
            got = swap(v, 2)
            if k == 0:
                return [a + got.astype(f32)] + far
            v = (a + got.astype(f32)).astype(bf16)
            far.append(swap(v, 2 * k))

    _, weighted, gram = finish(*forward(omega, True), weights, float(params))
    pieces = backward(weighted)
    inv_one = inverse_factor(gram_sum(gram), total_rows)
    back = small_call(functools.partial(back_kernel, float(total_rows) ** -0.5),
                      jax.ShapeDtypeStruct((columns, block), bf16), [inv_one] + pieces)
    second, weighted, gram = finish(*forward(back, False), weights, None)
    pieces = backward(weighted)
    inv_two = inverse_factor(gram_sum(gram), total_rows)
    range_basis = lax.dot_general(second[:, :rows], inv_two, (((0,), (1,)), ((), ())), precision=HIGH)
    coefficients = small_call(functools.partial(project_kernel, float(total_rows) ** -0.5),
                              jax.ShapeDtypeStruct((length, columns, strike), f32), [inv_two] + pieces)
    return (range_basis, coefficients.transpose(0, 2, 1))


def solution(mesh):
    in_specs = (P(("grp", "row"), None), P(("grp", "row")), P("grp"), P("grp", "row", None))
    out_specs = (P(("grp", "row"), None), P(("grp", "row"), None, None))

    return jax.shard_map(local, mesh=mesh, in_specs=in_specs, out_specs=out_specs, check_vma=False)
```
